256 devices in a mesh: dp: 64 (over y, z, core), rep: 4 (over x).
Axes of the slice: x: 4, y: 4, z: 8, core: 2. Of those that a mesh axis runs over, the one named last changes fastest.
Arguments:
- item_table: bfloat16 [32768, 512], P(('dp', 'rep')), may hold values from -6 to 6
- requests: int32 [256, 256, 2], P(('dp', 'rep')), may hold values from 0 to 127, as said below
- event_slot: int32 [131072], P(('dp', 'rep')), may hold values from 0 to 511, as said below
- lengths: int32 [256, 4], P(('dp', 'rep')), may hold values from 1 to 256, 512 in all within a row
- leaf_ids: int32 [131072, 8], P(('dp', 'rep')), may hold values from 0 to 31
- leaf_table: bfloat16 [256, 512], replicated, may hold values from -2.09375 to 2.09375
- w_in: bfloat16 [512, 2048], replicated, may hold values from -0.25 to 0.25
- w_out: bfloat16 [512, 512], replicated, may hold values from -0.25 to 0.25
- cotangent: bfloat16 [131072, 512], P(('dp', 'rep')), may hold values from -6 to 6
Outputs:
- output: bfloat16 [131072, 512], P(('dp', 'rep'))
- table_grad: float32 [32768, 512], P(('dp', 'rep'))
- leaf_grad: float32 [256, 512], replicated
- w_in_grad: float32 [512, 2048], replicated
- w_out_grad: float32 [512, 512], replicated
The draws below stay inside these ranges and needn't reach their ends.
Inputs may be any that keep to these rules, and one draw needn't show every extreme that they name: `requests`: for each device and owner the 2 requested rows are distinct. `event_slot`: every one of a device's 512 slots is named by at least one of its events.
All inputs are finite; a program needn't handle non-finite values.
Results may differ from the reference program's by a relative error of at most 0.014.
Values may be sent and summed in bfloat16 or wider, within the bound.
A program may use at most 64 MiB of HBM per device.

```python
import math
import jax
import jax.numpy as jnp
import numpy as np
from jax import lax

D = 512
HEADS = 4
TREES = 8
LEAVES = 32
CAP = 2
TOK_DEV = 512
MAXLEN = 256
SEQS_DEV = 4
SLOTS = 512
ROWS_DEV = 128
ROWS = 32768
TOKENS = 131072
DEVICES = 256


def draw_requests(key, part):
    first_key, second_key = jax.random.split(key)
    starts = jax.random.randint(first_key, (DEVICES, DEVICES, 1), 0, ROWS_DEV)
    starts = starts.at[0, 0, 0].set(ROWS_DEV - 1).at[0, 1, 0].set(0)
    strides = 2 * jax.random.randint(second_key, (DEVICES, DEVICES, 1), 0, ROWS_DEV // 2) + 1
    offsets = jnp.arange(CAP, dtype=jnp.int32)[None, None, :]
    return ((starts + offsets * strides) % ROWS_DEV).astype(jnp.int32)


def draw_event_slot(key, part):
    device_keys = jax.random.split(key, DEVICES)

    def one_device(device_key):
        extra_key, order_key = jax.random.split(device_key)
        extra = jax.random.randint(extra_key, (TOK_DEV - SLOTS,), 0, SLOTS)
        listing = jnp.concatenate([jnp.arange(SLOTS, dtype=jnp.int32), extra.astype(jnp.int32)])
        return jax.random.permutation(order_key, listing)
    return jax.vmap(one_device)(device_keys).reshape(-1).astype(jnp.int32)


def with_ends(entries, rng, least, high):
    longest = entries.shape.index(max(entries.shape))
    spots = []
    for shift in (0, 1):
        where = [jax.random.randint(jax.random.fold_in(rng, axis), (), 0, length) for axis, length in enumerate(entries.shape)]
        where[longest] = (where[longest] + shift) % entries.shape[longest]
        spots.append(tuple(where))
    return entries.at[spots[0]].set(least).at[spots[1]].set(high)


def levels(rng, extent, cuts, smallest, high):
    level = 1.0
    for axis_at, shards_of in cuts:
        heights = jax.random.uniform(jax.random.fold_in(jax.random.fold_in(rng, 6), axis_at), (shards_of,), jnp.float32, smallest / len(cuts), high / len(cuts))
        level = level * jnp.repeat(jnp.exp(heights), extent[axis_at] // shards_of).reshape((-1,) + (1,) * (len(extent) - 1 - axis_at))
    return level


def split_up(count, total, reach, slope):
    weights = [(1 << 20) // math.isqrt(rank ** slope) + 1 for rank in range(2, count + 1)]
    spare, counts = total - reach - (count - 1), [1] * (count - 1)
    while spare > 0:
        candidates = [i for i in range(count - 1) if counts[i] < reach]
        whole, remaining = sum([weights[i] for i in candidates]), spare
        for i in candidates:
            more = min(reach - counts[i], max(1, remaining * weights[i] // whole), spare)
            counts[i] = counts[i] + more
            spare = spare - more
    return np.array([reach] + counts)


def uneven(stream_key, amount, total, most, lean):
    if amount == 2:
        one = jax.random.randint(stream_key, (), max(1, total - most), min(most, total - 1) + 1)
        return jnp.stack([one, total - one])
    sizes = jnp.asarray(split_up(amount, total, most, lean), jnp.int32)
    pairs = (amount - 1) // 2
    donor, taker = sizes[1:1 + 2 * pairs:2], sizes[2:2 + 2 * pairs:2]
    margin = jnp.minimum(donor - 1, most - taker)
    moved = jax.random.randint(jax.random.fold_in(stream_key, 1), (pairs,), 0, 1 << 20) % (margin + 1)
    sizes = sizes.at[1:1 + 2 * pairs:2].set(donor - moved).at[2:2 + 2 * pairs:2].set(taker + moved)
    return sizes[jax.random.permutation(jax.random.fold_in(stream_key, 2), amount)]


def gaussian(key, dims, scale, bound, cuts=(), kind=jnp.bfloat16):
    gain = levels(key, dims, cuts, -0.22, 0.18) if cuts else 1.0
    values = jax.random.normal(key, dims, jnp.float32) * scale * gain
    return jnp.minimum(jnp.maximum(values, -bound), bound).astype(kind)


def setup_inputs(seed: int = 0) -> dict:
    splits = jax.random.split(jax.random.key(seed), 10)
    return {
        "item_table": gaussian(splits[0], (ROWS, D), 1.0, 6.0, ((0, 256),)),
        "requests": draw_requests(jax.random.fold_in(splits[9], 71), 0),
        "event_slot": draw_event_slot(jax.random.fold_in(splits[9], 71), 0),
        "lengths": jax.vmap(lambda own: uneven(own, SEQS_DEV, TOK_DEV, MAXLEN, 2))(jax.random.split(splits[3], DEVICES)).reshape((DEVICES, SEQS_DEV)).astype(jnp.int32),
        "leaf_ids": with_ends(jax.random.randint(splits[4], (TOKENS, TREES), 0, LEAVES), jax.random.fold_in(splits[4], 1), 0, LEAVES - 1).astype(jnp.int32),
        "leaf_table": gaussian(splits[5], (TREES * LEAVES, D), 0.35, 2.09375),
        "w_in": gaussian(splits[6], (D, 4 * D), D ** -0.5, 0.25),
        "w_out": gaussian(splits[7], (D, D), D ** -0.5, 0.25),
        "cotangent": gaussian(splits[8], (TOKENS, D), 1.0, 6.0, ((0, 256),)),
    }


epsilon = 1e-06

def normalize(values):
    center = values - lax.optimization_barrier(jnp.mean(values, axis=-1, keepdims=True))
    spread = lax.optimization_barrier(jnp.mean(center * center, axis=-1, keepdims=True))
    return center * lax.rsqrt(spread + epsilon)

def visible(lengths, count):
    ends = jnp.cumsum(lengths)
    places = jnp.arange(count, dtype=jnp.int32)
    segment = lax.optimization_barrier(jnp.sum((places[:, None] >= ends[None, :]).astype(jnp.int32), axis=1))
    same = segment[:, None] == segment[None, :]
    return jnp.logical_and(same, places[None, :] <= places[:, None])

def front(rows, event_slot, lengths, leaf_ids, leaf_table, w_in):
    count = event_slot.shape[0]
    picker = (event_slot[:, None] == jnp.arange(rows.shape[0], dtype=jnp.int32)[None, :]).astype(jnp.bfloat16)
    leaves = leaf_table.shape[0] // leaf_ids.shape[1]
    onehot = (leaf_ids[:, :, None] == jnp.arange(leaves, dtype=jnp.int32)[None, None, :]).reshape(count, -1).astype(jnp.bfloat16)
    inputs = (jnp.dot(picker, rows, preferred_element_type=jnp.float32) + jnp.dot(onehot, leaf_table, preferred_element_type=jnp.float32)).astype(jnp.bfloat16)
    normed = normalize(inputs.astype(jnp.float32)).astype(jnp.bfloat16)
    hidden = jax.nn.silu(jnp.dot(normed, w_in, preferred_element_type=jnp.float32)).astype(jnp.bfloat16)
    width = w_in.shape[0]
    head_size = width // HEADS
    gates = hidden[:, 0:width]
    value_heads = hidden[:, width:2 * width].reshape(count, HEADS, head_size)
    query_heads = hidden[:, 2 * width:3 * width].reshape(count, HEADS, head_size)
    key_heads = hidden[:, 3 * width:4 * width].reshape(count, HEADS, head_size)
    scores = jnp.einsum('qhd,khd->hqk', query_heads.astype(jnp.float32), key_heads.astype(jnp.float32)) * head_size ** (-0.5)
    allowed = visible(lengths, count)
    weights = jnp.where(allowed[None], jax.nn.silu(scores), 0.0).astype(jnp.bfloat16)
    mixed = jnp.einsum('hqk,khd->qhd', weights.astype(jnp.float32), value_heads.astype(jnp.float32)).reshape(count, width)
    gated = (normalize(mixed) * gates.astype(jnp.float32)).astype(jnp.bfloat16)
    return (inputs, gated)

def back(inputs, gated, w_out):
    return (jnp.dot(gated, w_out, preferred_element_type=jnp.float32) + inputs.astype(jnp.float32)).astype(jnp.bfloat16)

def reference(item_table, requests, event_slot, lengths, leaf_ids, leaf_table, w_in, w_out, cotangent):
    owner_rows = item_table.reshape(DEVICES, ROWS_DEV, D)
    owners = jnp.arange(DEVICES, dtype=jnp.int32)[None, :, None]
    fetched = owner_rows[owners, requests].reshape(DEVICES, SLOTS, D)

    def one_device(carry, items):
        rows, slots, history, leaf_rows, tangent = items

        def local_front(arrived, table_leaf, weight_in):
            return front(arrived, slots, history, leaf_rows, table_leaf, weight_in)
        (inputs, gated), pull_front = jax.vjp(local_front, rows, leaf_table, w_in)
        output, pull_back = jax.vjp(back, inputs, gated, w_out)
        d_inputs, d_gated, d_out = pull_back(tangent)
        d_rows, d_leaf, d_in = pull_front((d_inputs, d_gated))
        carry = (carry[0] + d_leaf.astype(jnp.float32), carry[1] + d_in.astype(jnp.float32), carry[2] + d_out.astype(jnp.float32))
        return (carry, (output, d_rows))
    start = (jnp.zeros(leaf_table.shape, jnp.float32), jnp.zeros(w_in.shape, jnp.float32), jnp.zeros(w_out.shape, jnp.float32))
    items = (fetched, event_slot.reshape(DEVICES, TOK_DEV), lengths, leaf_ids.reshape(DEVICES, TOK_DEV, TREES), cotangent.reshape(DEVICES, TOK_DEV, D))
    sums, stacked = lax.scan(one_device, start, items)
    outputs, row_grads = stacked
    flat_index = (owners * ROWS_DEV + requests).reshape(-1).astype(jnp.int32)
    table_grad = jnp.zeros((ROWS, D), jnp.float32).at[flat_index].add(row_grads.reshape(-1, D).astype(jnp.float32))
    share = 1.0 / DEVICES
    return (outputs.reshape(TOKENS, D), table_grad, sums[0] * share, sums[1] * share, sums[2] * share)
```

```python
import jax
import jax.numpy as jnp
from jax import lax
from jax.experimental import pallas as pl
from jax.experimental.pallas import tpu as pltpu
from jax.sharding import PartitionSpec as P

HEADS = 4


epsilon = 1e-06


def normalize(values):
    center = values - jnp.mean(values, axis=-1, keepdims=True)
    spread = jnp.mean(center * center, axis=-1, keepdims=True)
    return center * lax.rsqrt(spread + epsilon)


def visible(lengths, count):
    ends = jnp.cumsum(lengths)
    places = jnp.arange(count, dtype=jnp.int32)
    segment = jnp.sum((places[:, None] >= ends[None, :]).astype(jnp.int32), axis=1)
    same = segment[:, None] == segment[None, :]
    return jnp.logical_and(same, places[None, :] <= places[:, None])


def front(rows, event_slot, lengths, leaf_ids, leaf_table, w_in):
    count = event_slot.shape[0]
    picker = (event_slot[:, None] == jnp.arange(rows.shape[0], dtype=jnp.int32)[None, :]).astype(
        jnp.bfloat16
    )
    leaves = leaf_table.shape[0] // leaf_ids.shape[1]
    onehot = (
        (leaf_ids[:, :, None] == jnp.arange(leaves, dtype=jnp.int32)[None, None, :])
        .reshape(count, -1)
        .astype(jnp.bfloat16)
    )
    inputs = (
        jnp.dot(picker, rows, preferred_element_type=jnp.float32)
        + jnp.dot(onehot, leaf_table, preferred_element_type=jnp.float32)
    ).astype(jnp.bfloat16)
    normed = normalize(inputs.astype(jnp.float32)).astype(jnp.bfloat16)
    hidden = jax.nn.silu(jnp.dot(normed, w_in, preferred_element_type=jnp.float32)).astype(
        jnp.bfloat16
    )
    width = w_in.shape[0]
    head_size = width // HEADS
    gates = hidden[:, 0:width]
    value_heads = hidden[:, width : 2 * width].reshape(count, HEADS, head_size)
    query_heads = hidden[:, 2 * width : 3 * width].reshape(count, HEADS, head_size)
    key_heads = hidden[:, 3 * width : 4 * width].reshape(count, HEADS, head_size)
    scores = jnp.einsum(
        "qhd,khd->hqk", query_heads, key_heads, preferred_element_type=jnp.float32
    ) * head_size ** (-0.5)
    allowed = visible(lengths, count)
    weights = jnp.where(allowed[None], jax.nn.silu(scores), 0.0).astype(jnp.bfloat16)
    mixed = jnp.einsum(
        "hqk,khd->qhd", weights, value_heads, preferred_element_type=jnp.float32
    ).reshape(count, width)
    gated = (normalize(mixed) * gates.astype(jnp.float32)).astype(jnp.bfloat16)
    return (inputs, gated)


def back(inputs, gated, w_out):
    return (
        jnp.dot(gated, w_out, preferred_element_type=jnp.float32) + inputs.astype(jnp.float32)
    ).astype(jnp.bfloat16)


def send_asked(wanted):
    result = lax.all_to_all(
        lax.all_to_all(wanted, "dp", split_axis=0, concat_axis=0, tiled=True),
        "rep",
        split_axis=1,
        concat_axis=1,
        tiled=True,
    )
    return result


def send_fetched(fetched):
    result = lax.all_to_all(
        lax.all_to_all(fetched, "dp", split_axis=0, concat_axis=0, tiled=True),
        "rep",
        split_axis=1,
        concat_axis=1,
        tiled=True,
    )
    return result


def send_returned(gradients):
    result = lax.all_to_all(
        lax.all_to_all(gradients, "dp", split_axis=0, concat_axis=0, tiled=True),
        "rep",
        split_axis=1,
        concat_axis=1,
        tiled=True,
    )
    return result


MESH = pl.DeviceIdType.MESH
ROWS_ALL = 3072
HALF = 1536
R1 = 384
R2 = 96
RZ = 48


def here():
    dp = lax.axis_index("dp")
    x = lax.axis_index("rep")
    c = lax.rem(dp, 2)
    z = lax.rem(dp // 2, 8)
    y = dp // 16
    return x, y, z, c


def device(x, y, z, c):
    return ((y * 8 + z) * 2 + c, x)


def span(start, size):
    return pl.ds(pl.multiple_of(start, size), size)


def add_into(dst, start, sources, rows, step):
    def body(i, carry):
        total = None
        for ref, first in sources:
            part = ref[pl.ds(pl.multiple_of(first + i * step, 16), step), :].astype(jnp.float32)
            total = part if total is None else total + part
        dst[pl.ds(pl.multiple_of(start + i * step, 16), step), :] = total.astype(dst.dtype)
        return carry

    lax.fori_loop(0, rows // step, body, 0)


def sum_kernel(g, out, w, r0, r1a, r1b, r2a, r2b, rz, ssem, rsem):
    x, y, z, c = here()
    p1 = (1 - c) * x + c * y
    p2 = c * x + (1 - c) * y

    def axis1(d):
        return device(lax.rem(x + (1 - c) * d, 4), lax.rem(y + c * d, 4), z, c)

    def axis2(d):
        return device(lax.rem(x + c * d, 4), lax.rem(y + (1 - c) * d, 4), z, c)

    def axisz(d):
        return device(x, y, lax.rem(z + d, 8), c)

    partner = device(x, y, z, 1 - c)
    barrier = pltpu.get_barrier_semaphore()
    peers = [partner, axis1(1), axis1(3), axis2(1), axis2(3)] + [axisz(j) for j in range(1, 8)]
    for peer in peers:
        pl.semaphore_signal(barrier, inc=1, device_id=peer, device_id_type=MESH)
    pl.semaphore_wait(barrier, len(peers))

    started = []

    def send(src, dst, index, to):
        copy = pltpu.make_async_remote_copy(
            src_ref=src,
            dst_ref=dst,
            send_sem=ssem.at[index],
            recv_sem=rsem.at[index],
            device_id=to,
            device_id_type=MESH,
        )
        copy.start()
        started.append(copy)

    def arrive(ref, index):
        pltpu.make_async_remote_copy(
            src_ref=ref,
            dst_ref=ref,
            send_sem=ssem.at[index],
            recv_sem=rsem.at[index],
            device_id=partner,
            device_id_type=MESH,
        ).wait_recv()

    base = c * HALF
    other = (1 - c) * HALF
    order = (2, 1, 3, 0)
    for k, off in enumerate(order):
        q = lax.rem(p2 + off, 4)
        send(g.at[span(other + q * R1, R1), :], r0.at[span(q * R1, R1), :], k, partner)

    def ring_sum(pos, first, rows, right, left, ra, rb, index, local, own):
        half = rows // 2
        q2 = lax.rem(pos + 2, 4)
        q1 = lax.rem(pos + 1, 4)
        q3 = lax.rem(pos + 3, 4)
        local(q2, 0)
        at = first + q2 * rows
        send(w.at[span(at, half), :], ra.at[0], index, right)
        send(w.at[span(at + half, half), :], ra.at[1], index + 1, left)
        local(q1, 1)
        local(q3, 2)
        arrive(ra.at[0], index)
        at = first + q1 * rows
        add_into(w, at, [(w, at), (ra.at[0], 0)], half, 48)
        send(w.at[span(at, rows), :], rb.at[0], index + 2, right)
        arrive(ra.at[1], index + 1)
        at = first + q3 * rows
        add_into(w, at + half, [(w, at + half), (ra.at[1], 0)], half, 48)
        send(w.at[span(at, rows), :], rb.at[1], index + 3, left)
        own()
        arrive(rb.at[0], index + 2)
        arrive(rb.at[1], index + 3)

    def local1(q, k):
        at = q * R1
        arrive(r0.at[span(at, R1), :], k)
        add_into(w, at, [(g, base + at), (r0, at)], R1, 48)

    w1 = p1 * R1
    ring_sum(
        p1, 0, R1, axis1(1), axis1(3), r1a, r1b, 4, local1,
        lambda: arrive(r0.at[span(w1, R1), :], 3),
    )
    add_into(w, w1, [(g, base + w1), (r0, w1), (r1b.at[0], 0), (r1b.at[1], 0)], R1, 48)
    w2 = w1 + p2 * R2
    ring_sum(
        p2, w1, R2, axis2(1), axis2(3), r2a, r2b, 8, lambda q, k: None, lambda: None
    )
    add_into(w, w2, [(w, w2), (r2b.at[0], 0), (r2b.at[1], 0)], R2, 48)

    def part(j):
        return j // 4 * RZ, lax.rem(j, 4) * 128

    for j in range(1, 8):
        row, column = part(lax.rem(z + j, 8))
        send(
            w.at[pl.ds(pl.multiple_of(w2 + row, RZ), RZ), span(column, 128)],
            rz.at[j - 1],
            11 + j,
            axisz(j),
        )
    row, column = part(z)
    total = w[pl.ds(pl.multiple_of(w2 + row, RZ), RZ), span(column, 128)].astype(jnp.float32)
    for j in range(1, 8):
        arrive(rz.at[j - 1], 11 + j)
        total = total + rz[j - 1].astype(jnp.float32)
    mine = (pl.ds(pl.multiple_of(base + w2 + row, RZ), RZ), span(column, 128))
    out[mine] = total.astype(out.dtype)
    for j in range(1, 8):
        send(out.at[mine], out.at[mine], 18 + j, axisz(j))
    for j in range(1, 8):
        row, column = part(lax.rem(z + 8 - j, 8))
        arrive(out.at[pl.ds(pl.multiple_of(base + w2 + row, RZ), RZ), span(column, 128)], 18 + j)

    def ring_share(pos, first, rows, right, left, index, ready):
        half = rows // 2
        at = first + pos * rows
        send(out.at[span(at, rows), :], out.at[span(at, rows), :], index, right)
        send(out.at[span(at, rows), :], out.at[span(at, rows), :], index + 1, left)
        ready(pos, 0)
        q = lax.rem(pos + 3, 4)
        at = first + q * rows
        arrive(out.at[span(at, rows), :], index)
        send(out.at[span(at, half), :], out.at[span(at, half), :], index + 2, right)
        ready(q, 1)
        q = lax.rem(pos + 1, 4)
        at = first + q * rows
        arrive(out.at[span(at, rows), :], index + 1)
        send(out.at[span(at + half, half), :], out.at[span(at + half, half), :], index + 3, left)
        ready(q, 2)
        q = lax.rem(pos + 2, 4)
        at = first + q * rows
        arrive(out.at[span(at, half), :], index + 2)
        arrive(out.at[span(at + half, half), :], index + 3)
        ready(q, 3)

    ring_share(p2, base + w1, R2, axis2(1), axis2(3), 26, lambda q, k: None)

    def pass_on(q, k):
        rows = out.at[span(base + q * R1, R1), :]
        send(rows, rows, 34 + k, partner)

    ring_share(p1, base, R1, axis1(1), axis1(3), 30, pass_on)
    for k, off in enumerate((0, 3, 1, 2)):
        q = lax.rem(p2 + off, 4)
        arrive(out.at[span(other + q * R1, R1), :], 34 + k)
    for copy in started:
        copy.wait_send()


def sum_all(g):
    vmem = pl.BlockSpec(memory_space=pltpu.VMEM)
    bf16 = jnp.bfloat16
    return pl.pallas_call(
        sum_kernel,
        out_shape=jax.ShapeDtypeStruct((ROWS_ALL, 512), bf16),
        in_specs=[vmem],
        out_specs=vmem,
        scratch_shapes=[
            pltpu.VMEM((HALF, 512), bf16),
            pltpu.VMEM((HALF, 512), bf16),
            pltpu.VMEM((2, R1 // 2, 512), bf16),
            pltpu.VMEM((2, R1, 512), bf16),
            pltpu.VMEM((2, R2 // 2, 512), bf16),
            pltpu.VMEM((2, R2, 512), bf16),
            pltpu.VMEM((7, RZ, 128), bf16),
            pltpu.SemaphoreType.DMA((38,)),
            pltpu.SemaphoreType.DMA((38,)),
        ],
        compiler_params=pltpu.CompilerParams(collective_id=0, has_side_effects=True),
    )(g)


def on_device(
    item_table, requests, event_slot, lengths, leaf_ids, leaf_table, w_in, w_out, cotangent
):
    data_count = lax.axis_size("dp")
    replica_count = lax.axis_size("rep")
    width = item_table.shape[1]
    wanted = requests.reshape(data_count, replica_count, -1)
    asked = send_asked(wanted)
    fetched = item_table[asked]
    arrived = send_fetched(fetched).reshape(-1, width)

    def local_front(rows, table_leaf, weight_in):
        return front(rows, event_slot, lengths[0], leaf_ids, table_leaf, weight_in)

    (inputs, gated), pull_front = jax.vjp(local_front, arrived, leaf_table, w_in)
    output, pull_back = jax.vjp(back, inputs, gated, w_out)
    d_inputs, d_gated, d_out = pull_back(cotangent)
    d_rows, d_leaf, d_in = pull_front((d_inputs, d_gated))
    returned = send_returned(d_rows.reshape(data_count, replica_count, -1, width))
    stacked = jnp.concatenate(
        [d_in[:, i * width : (i + 1) * width] for i in range(4)]
        + [d_out, d_leaf, jnp.zeros((ROWS_ALL - 2816, width), jnp.bfloat16)]
    )
    sums = sum_all(stacked).astype(jnp.float32)
    in_sum = jnp.concatenate([sums[i * width : (i + 1) * width] for i in range(4)], axis=1)
    out_sum = sums[2048:2560]
    leaf_sum = sums[2560:2816]
    table_grad = (
        jnp.zeros(item_table.shape, jnp.float32)
        .at[asked.reshape(-1)]
        .add(returned.reshape(-1, width).astype(jnp.float32))
    )
    share = 1.0 / (data_count * replica_count)
    return (output, table_grad, leaf_sum * share, in_sum * share, out_sum * share)


def solution(mesh):
    return jax.shard_map(
        on_device,
        mesh=mesh,
        in_specs=(
            P(("dp", "rep"), None),
            P(("dp", "rep"), None, None),
            P(("dp", "rep")),
            P(("dp", "rep"), None),
            P(("dp", "rep"), None),
            P(),
            P(),
            P(),
            P(("dp", "rep"), None),
        ),
        out_specs=(P(("dp", "rep"), None), P(("dp", "rep"), None), P(), P(), P()),
        check_vma=False,
    )
```

```python
import jax
import jax.numpy as jnp
from jax import lax
from jax.experimental import pallas as pl
from jax.experimental.pallas import tpu as pltpu
from jax.sharding import PartitionSpec as P

HEADS = 4


epsilon = 1e-06


def normalize(values):
    center = values - jnp.mean(values, axis=-1, keepdims=True)
    spread = jnp.mean(center * center, axis=-1, keepdims=True)
    return center * lax.rsqrt(spread + epsilon)


def visible(lengths, count):
    ends = jnp.cumsum(lengths)
    places = jnp.arange(count, dtype=jnp.int32)
    segment = jnp.sum((places[:, None] >= ends[None, :]).astype(jnp.int32), axis=1)
    same = segment[:, None] == segment[None, :]
    return jnp.logical_and(same, places[None, :] <= places[:, None])


def front(rows, event_slot, lengths, leaf_ids, leaf_table, w_in):
    count = event_slot.shape[0]
    picker = (event_slot[:, None] == jnp.arange(rows.shape[0], dtype=jnp.int32)[None, :]).astype(
        jnp.bfloat16
    )
    leaves = leaf_table.shape[0] // leaf_ids.shape[1]
    onehot = (
        (leaf_ids[:, :, None] == jnp.arange(leaves, dtype=jnp.int32)[None, None, :])
        .reshape(count, -1)
        .astype(jnp.bfloat16)
    )
    inputs = (
        jnp.dot(picker, rows, preferred_element_type=jnp.float32)
        + jnp.dot(onehot, leaf_table, preferred_element_type=jnp.float32)
    ).astype(jnp.bfloat16)
    normed = normalize(inputs.astype(jnp.float32)).astype(jnp.bfloat16)
    hidden = jax.nn.silu(jnp.dot(normed, w_in, preferred_element_type=jnp.float32)).astype(
        jnp.bfloat16
    )
    width = w_in.shape[0]
    head_size = width // HEADS
    gates = hidden[:, 0:width]
    value_heads = hidden[:, width : 2 * width].reshape(count, HEADS, head_size)
    query_heads = hidden[:, 2 * width : 3 * width].reshape(count, HEADS, head_size)
    key_heads = hidden[:, 3 * width : 4 * width].reshape(count, HEADS, head_size)
    scores = jnp.einsum(
        "qhd,khd->hqk", query_heads, key_heads, preferred_element_type=jnp.float32
    ) * head_size ** (-0.5)
    allowed = visible(lengths, count)
    weights = jnp.where(allowed[None], jax.nn.silu(scores), 0.0).astype(jnp.bfloat16)
    mixed = jnp.einsum(
        "hqk,khd->qhd", weights, value_heads, preferred_element_type=jnp.float32
    ).reshape(count, width)
    gated = (normalize(mixed) * gates.astype(jnp.float32)).astype(jnp.bfloat16)
    return (inputs, gated)


def back(inputs, gated, w_out):
    return (
        jnp.dot(gated, w_out, preferred_element_type=jnp.float32) + inputs.astype(jnp.float32)
    ).astype(jnp.bfloat16)


MESH = pl.DeviceIdType.MESH
ROWS_ALL = 3072
HALF = 1536
R1 = 384
R2 = 96
RZ = 48


def here():
    dp = lax.axis_index("dp")
    x = lax.axis_index("rep")
    c = lax.rem(dp, 2)
    z = lax.rem(dp // 2, 8)
    y = dp // 16
    return x, y, z, c


def device(x, y, z, c):
    return ((y * 8 + z) * 2 + c, x)


def span(start, size):
    return pl.ds(pl.multiple_of(start, size), size)


BLOCK = 128


def seat(t):
    return (t // 4, lax.rem(t, 4))


def greet_all(me, count):
    barrier = pltpu.get_barrier_semaphore()

    def body(j, carry):
        to = seat(lax.rem(me + j, count))
        pl.semaphore_signal(barrier, inc=1, device_id=to, device_id_type=MESH)
        return carry

    lax.fori_loop(1, count, body, 0)
    pl.semaphore_wait(barrier, count - 1)


def row_numbers(asked, first, sources):
    count = asked.shape[0]
    rows = sources * 8
    lanes = asked.shape[-1]
    table = asked.reshape(count, lanes).astype(jnp.float32).astype(jnp.bfloat16)
    row = lax.broadcasted_iota(jnp.int32, (rows, count), 0) // 8 + first
    source = lax.broadcasted_iota(jnp.int32, (rows, count), 1)
    spread = jnp.where(row == source, 1.0, 0.0).astype(jnp.bfloat16)
    both = jnp.dot(spread, table, preferred_element_type=jnp.float32)
    slot = lax.rem(lax.broadcasted_iota(jnp.int32, (rows, lanes), 0), 8) // 4
    lane = lax.broadcasted_iota(jnp.int32, (rows, lanes), 1)
    one = jnp.where(slot == lane, both, 0.0).astype(jnp.bfloat16)
    ones = jnp.ones((lanes, lanes), jnp.bfloat16)
    return jnp.dot(one, ones, preferred_element_type=jnp.float32)


def pickers(numbers):
    rows, lanes = numbers.shape
    lane = lax.broadcasted_iota(jnp.int32, (rows, lanes), 1).astype(jnp.float32)
    quarter = lax.rem(lax.broadcasted_iota(jnp.int32, (rows, lanes), 0), 4)
    hit = jnp.where(numbers == lane, 1.0, 0.0)
    return [jnp.where(quarter == k, hit, 0.0).astype(jnp.bfloat16) for k in range(4)]


def fetch_kernel(req, table, arrived, asked, fetched, ssem, rsem):
    count = req.shape[0]
    me = lax.axis_index("dp") * 4 + lax.axis_index("rep")
    greet_all(me, count)

    def copy(src, dst, index, to):
        return pltpu.make_async_remote_copy(
            src_ref=src,
            dst_ref=dst,
            send_sem=ssem.at[index],
            recv_sem=rsem.at[index],
            device_id=to,
            device_id_type=MESH,
        )

    def ask(j, carry):
        t = lax.rem(me + j, count)
        copy(req.at[t], asked.at[me], 0, seat(t)).start()
        return carry

    lax.fori_loop(1, count, ask, 0)
    asked[pl.ds(me, 1)] = req[pl.ds(me, 1)]
    every = asked.at[pl.ds(0, count - 1)]
    copy(every, every, 0, seat(me)).wait_recv()

    group = 32

    def serve(i, carry):
        first = lax.rem(me // group + i, count // group) * group
        hits = pickers(row_numbers(asked[...], first, group))
        rows = None
        for k in range(4):
            part = jnp.dot(
                hits[k], table[:, k * BLOCK : (k + 1) * BLOCK], preferred_element_type=jnp.float32
            )
            rows = part if rows is None else rows + part
        fetched[pl.ds(first, group)] = rows.reshape(group, 8, BLOCK).astype(jnp.bfloat16)

        def hand(j, inner):
            t = first + lax.rem(me + j, group)

            @pl.when(t != me)
            def _():
                copy(fetched.at[t], arrived.at[me], 1, seat(t)).start()

            return inner

        lax.fori_loop(0, group, hand, 0)
        return carry

    lax.fori_loop(0, count // group, serve, 0)
    arrived[pl.ds(me, 1)] = fetched[pl.ds(me, 1)]
    every = req.at[pl.ds(0, count - 1)]
    copy(every, every, 0, seat(me)).wait_send()
    every = arrived.at[pl.ds(0, count - 1)]
    copy(every, every, 1, seat(me)).wait_recv()
    every = fetched.at[pl.ds(0, count - 1)]
    copy(every, every, 1, seat(me)).wait_send()


def fetch_rows(req, table):
    vmem = pl.BlockSpec(memory_space=pltpu.VMEM)
    count = req.shape[0]
    return pl.pallas_call(
        fetch_kernel,
        out_shape=(
            jax.ShapeDtypeStruct((count, 8, BLOCK), jnp.bfloat16),
            jax.ShapeDtypeStruct((count, 1, BLOCK), jnp.int32),
        ),
        in_specs=[vmem, vmem],
        out_specs=(vmem, vmem),
        scratch_shapes=[
            pltpu.VMEM((count, 8, BLOCK), jnp.bfloat16),
            pltpu.SemaphoreType.DMA((2,)),
            pltpu.SemaphoreType.DMA((2,)),
        ],
        compiler_params=pltpu.CompilerParams(collective_id=1, has_side_effects=True),
    )(req, table)


def finish_kernel(sums, returned, asked, table_out, leaf_out, in_out, out_out):
    count = asked.shape[0]
    share = 1.0 / count
    group = 64
    table_out[...] = jnp.zeros_like(table_out)

    def gather(i, carry):
        first = i * group
        hits = pickers(row_numbers(asked[...], first, group))
        rows = returned[pl.ds(first, group)].reshape(group * 8, BLOCK)
        for k in range(4):
            table_out[:, k * BLOCK : (k + 1) * BLOCK] += lax.dot_general(
                hits[k], rows, (((0,), (0,)), ((), ())), preferred_element_type=jnp.float32
            )
        return carry

    lax.fori_loop(0, count // group, gather, 0)
    width = 512

    def scale(first, dst, rows, column):
        def body(i, carry):
            at = pl.multiple_of(i * 64, 64)
            dst[pl.ds(at, 64), column : column + width] = (
                sums[pl.ds(pl.multiple_of(first + i * 64, 64), 64), :].astype(jnp.float32) * share
            )
            return carry

        lax.fori_loop(0, rows // 64, body, 0)

    for i in range(4):
        scale(i * width, in_out, width, i * width)
    scale(2048, out_out, 512, 0)
    scale(2560, leaf_out, 256, 0)


def finish(sums, returned, asked):
    vmem = pl.BlockSpec(memory_space=pltpu.VMEM)
    f32 = jnp.float32
    return pl.pallas_call(
        finish_kernel,
        out_shape=(
            jax.ShapeDtypeStruct((128, 512), f32),
            jax.ShapeDtypeStruct((256, 512), f32),
            jax.ShapeDtypeStruct((512, 2048), f32),
            jax.ShapeDtypeStruct((512, 512), f32),
        ),
        in_specs=[vmem] * 3,
        out_specs=(vmem,) * 4,
    )(sums, returned, asked)


def add_into(dst, start, sources, rows, step):
    def body(i, carry):
        total = None
        for ref, first in sources:
            part = ref[pl.ds(pl.multiple_of(first + i * step, 16), step), :].astype(jnp.float32)
            total = part if total is None else total + part
        dst[pl.ds(pl.multiple_of(start + i * step, 16), step), :] = total.astype(dst.dtype)
        return carry

    lax.fori_loop(0, rows // step, body, 0)


def sum_kernel(g, back, out, returned, w, r0, r1a, r1b, r2a, r2b, rz, ssem, rsem, bsem):
    x, y, z, c = here()
    p1 = (1 - c) * x + c * y
    p2 = c * x + (1 - c) * y

    def axis1(d):
        return device(lax.rem(x + (1 - c) * d, 4), lax.rem(y + c * d, 4), z, c)

    def axis2(d):
        return device(lax.rem(x + c * d, 4), lax.rem(y + (1 - c) * d, 4), z, c)

    def axisz(d):
        return device(x, y, lax.rem(z + d, 8), c)

    partner = device(x, y, z, 1 - c)
    count = back.shape[0]
    me = lax.axis_index("dp") * 4 + x
    greet_all(me, count)

    started = []

    def send(src, dst, index, to):
        copy = pltpu.make_async_remote_copy(
            src_ref=src,
            dst_ref=dst,
            send_sem=ssem.at[index],
            recv_sem=rsem.at[index],
            device_id=to,
            device_id_type=MESH,
        )
        copy.start()
        started.append(copy)

    def arrive(ref, index):
        pltpu.make_async_remote_copy(
            src_ref=ref,
            dst_ref=ref,
            send_sem=ssem.at[index],
            recv_sem=rsem.at[index],
            device_id=partner,
            device_id_type=MESH,
        ).wait_recv()

    base = c * HALF
    other = (1 - c) * HALF
    order = (2, 1, 3, 0)
    for k, off in enumerate(order):
        q = lax.rem(p2 + off, 4)
        send(g.at[span(other + q * R1, R1), :], r0.at[span(q * R1, R1), :], k, partner)

    def back_copy(src, dst, to):
        return pltpu.make_async_remote_copy(
            src_ref=src,
            dst_ref=dst,
            send_sem=bsem.at[0],
            recv_sem=bsem.at[1],
            device_id=to,
            device_id_type=MESH,
        )

    def give_back(j, carry):
        t = lax.rem(me + j, count)
        back_copy(back.at[t], returned.at[me], seat(t)).start()
        return carry

    lax.fori_loop(1, count, give_back, 0)
    returned[pl.ds(me, 1)] = back[pl.ds(me, 1)]

    def ring_sum(pos, first, rows, right, left, ra, rb, index, local, own):
        half = rows // 2
        q2 = lax.rem(pos + 2, 4)
        q1 = lax.rem(pos + 1, 4)
        q3 = lax.rem(pos + 3, 4)
        local(q2, 0)
        at = first + q2 * rows
        send(w.at[span(at, half), :], ra.at[0], index, right)
        send(w.at[span(at + half, half), :], ra.at[1], index + 1, left)
        local(q1, 1)
        local(q3, 2)
        arrive(ra.at[0], index)
        at = first + q1 * rows
        add_into(w, at, [(w, at), (ra.at[0], 0)], half, 48)
        send(w.at[span(at, rows), :], rb.at[0], index + 2, right)
        arrive(ra.at[1], index + 1)
        at = first + q3 * rows
        add_into(w, at + half, [(w, at + half), (ra.at[1], 0)], half, 48)
        send(w.at[span(at, rows), :], rb.at[1], index + 3, left)
        own()
        arrive(rb.at[0], index + 2)
        arrive(rb.at[1], index + 3)

    def local1(q, k):
        at = q * R1
        arrive(r0.at[span(at, R1), :], k)
        add_into(w, at, [(g, base + at), (r0, at)], R1, 48)

    w1 = p1 * R1
    ring_sum(
        p1, 0, R1, axis1(1), axis1(3), r1a, r1b, 4, local1,
        lambda: arrive(r0.at[span(w1, R1), :], 3),
    )
    add_into(w, w1, [(g, base + w1), (r0, w1), (r1b.at[0], 0), (r1b.at[1], 0)], R1, 48)
    w2 = w1 + p2 * R2
    ring_sum(
        p2, w1, R2, axis2(1), axis2(3), r2a, r2b, 8, lambda q, k: None, lambda: None
    )
    add_into(w, w2, [(w, w2), (r2b.at[0], 0), (r2b.at[1], 0)], R2, 48)

    def part(j):
        return j // 4 * RZ, lax.rem(j, 4) * 128

    for j in range(1, 8):
        row, column = part(lax.rem(z + j, 8))
        send(
            w.at[pl.ds(pl.multiple_of(w2 + row, RZ), RZ), span(column, 128)],
            rz.at[j - 1],
            11 + j,
            axisz(j),
        )
    row, column = part(z)
    total = w[pl.ds(pl.multiple_of(w2 + row, RZ), RZ), span(column, 128)].astype(jnp.float32)
    for j in range(1, 8):
        arrive(rz.at[j - 1], 11 + j)
        total = total + rz[j - 1].astype(jnp.float32)
    mine = (pl.ds(pl.multiple_of(base + w2 + row, RZ), RZ), span(column, 128))
    out[mine] = total.astype(out.dtype)
    for j in range(1, 8):
        send(out.at[mine], out.at[mine], 18 + j, axisz(j))
    for j in range(1, 8):
        row, column = part(lax.rem(z + 8 - j, 8))
        arrive(out.at[pl.ds(pl.multiple_of(base + w2 + row, RZ), RZ), span(column, 128)], 18 + j)

    def ring_share(pos, first, rows, right, left, index, ready):
        half = rows // 2
        at = first + pos * rows
        send(out.at[span(at, rows), :], out.at[span(at, rows), :], index, right)
        send(out.at[span(at, rows), :], out.at[span(at, rows), :], index + 1, left)
        ready(pos, 0)
        q = lax.rem(pos + 3, 4)
        at = first + q * rows
        arrive(out.at[span(at, rows), :], index)
        send(out.at[span(at, half), :], out.at[span(at, half), :], index + 2, right)
        ready(q, 1)
        q = lax.rem(pos + 1, 4)
        at = first + q * rows
        arrive(out.at[span(at, rows), :], index + 1)
        send(out.at[span(at + half, half), :], out.at[span(at + half, half), :], index + 3, left)
        ready(q, 2)
        q = lax.rem(pos + 2, 4)
        at = first + q * rows
        arrive(out.at[span(at, half), :], index + 2)
        arrive(out.at[span(at + half, half), :], index + 3)
        ready(q, 3)

    ring_share(p2, base + w1, R2, axis2(1), axis2(3), 26, lambda q, k: None)

    def pass_on(q, k):
        rows = out.at[span(base + q * R1, R1), :]
        send(rows, rows, 34 + k, partner)

    ring_share(p1, base, R1, axis1(1), axis1(3), 30, pass_on)
    for k, off in enumerate((0, 3, 1, 2)):
        q = lax.rem(p2 + off, 4)
        arrive(out.at[span(other + q * R1, R1), :], 34 + k)
    for copy in started:
        copy.wait_send()
    every = returned.at[pl.ds(0, count - 1)]
    back_copy(every, every, seat(me)).wait_recv()
    every = back.at[pl.ds(0, count - 1)]
    back_copy(every, every, seat(me)).wait_send()


def sum_all(g, back):
    vmem = pl.BlockSpec(memory_space=pltpu.VMEM)
    bf16 = jnp.bfloat16
    return pl.pallas_call(
        sum_kernel,
        out_shape=(
            jax.ShapeDtypeStruct((ROWS_ALL, 512), bf16),
            jax.ShapeDtypeStruct(back.shape, bf16),
        ),
        in_specs=[vmem, vmem],
        out_specs=(vmem, vmem),
        scratch_shapes=[
            pltpu.VMEM((HALF, 512), bf16),
            pltpu.VMEM((HALF, 512), bf16),
            pltpu.VMEM((2, R1 // 2, 512), bf16),
            pltpu.VMEM((2, R1, 512), bf16),
            pltpu.VMEM((2, R2 // 2, 512), bf16),
            pltpu.VMEM((2, R2, 512), bf16),
            pltpu.VMEM((7, RZ, 128), bf16),
            pltpu.SemaphoreType.DMA((38,)),
            pltpu.SemaphoreType.DMA((38,)),
            pltpu.SemaphoreType.DMA((2,)),
        ],
        compiler_params=pltpu.CompilerParams(collective_id=0, has_side_effects=True),
    )(g, back)


def on_device(
    item_table, requests, event_slot, lengths, leaf_ids, leaf_table, w_in, w_out, cotangent
):
    width = item_table.shape[1]
    count = requests.shape[1]
    asks = jnp.pad(requests.reshape(count, 1, 2), ((0, 0), (0, 0), (0, BLOCK - 2)))
    blocks, asked = fetch_rows(asks, item_table)
    arrived = blocks.reshape(-1, width)

    def local_front(rows, table_leaf, weight_in):
        return front(rows, event_slot, lengths[0], leaf_ids, table_leaf, weight_in)

    (inputs, gated), pull_front = jax.vjp(local_front, arrived, leaf_table, w_in)
    output, pull_back = jax.vjp(back, inputs, gated, w_out)
    d_inputs, d_gated, d_out = pull_back(cotangent)
    d_rows, d_leaf, d_in = pull_front((d_inputs, d_gated))
    stacked = jnp.concatenate(
        [d_in[:, i * width : (i + 1) * width] for i in range(4)]
        + [d_out, d_leaf, jnp.zeros((ROWS_ALL - 2816, width), jnp.bfloat16)]
    )
    sums, returned = sum_all(stacked, d_rows.reshape(blocks.shape))
    return (output, *finish(sums, returned, asked))


def solution(mesh):
    return jax.shard_map(
        on_device,
        mesh=mesh,
        in_specs=(
            P(("dp", "rep"), None),
            P(("dp", "rep"), None, None),
            P(("dp", "rep")),
            P(("dp", "rep"), None),
            P(("dp", "rep"), None),
            P(),
            P(),
            P(),
            P(("dp", "rep"), None),
        ),
        out_specs=(P(("dp", "rep"), None), P(("dp", "rep"), None), P(), P(), P()),
        check_vma=False,
    )
```

```python
import jax
import jax.numpy as jnp
from jax import lax
from jax.experimental import pallas as pl
from jax.experimental.pallas import tpu as pltpu
from jax.sharding import PartitionSpec as P

HEADS = 4


epsilon = 1e-06


MESH = pl.DeviceIdType.MESH
ROWS_ALL = 3072
HALF = 1536
R1 = 384
R2 = 96
RZ = 48


def here():
    dp = lax.axis_index("dp")
    x = lax.axis_index("rep")
    c = lax.rem(dp, 2)
    z = lax.rem(dp // 2, 8)
    y = dp // 16
    return x, y, z, c


def device(x, y, z, c):
    return ((y * 8 + z) * 2 + c, x)


def span(start, size):
    return pl.ds(pl.multiple_of(start, size), size)


BLOCK = 128


def seat(t):
    return (t // 4, lax.rem(t, 4))


def greet_all(me, count):
    barrier = pltpu.get_barrier_semaphore()

    def body(j, carry):
        to = seat(lax.rem(me + j, count))
        pl.semaphore_signal(barrier, inc=1, device_id=to, device_id_type=MESH)
        return carry

    lax.fori_loop(1, count, body, 0)
    pl.semaphore_wait(barrier, count - 1)


def row_numbers(asked, first, sources):
    count = asked.shape[0]
    rows = sources * 8
    lanes = asked.shape[-1]
    table = asked.reshape(count, lanes).astype(jnp.float32).astype(jnp.bfloat16)
    row = lax.broadcasted_iota(jnp.int32, (rows, count), 0) // 8 + first
    source = lax.broadcasted_iota(jnp.int32, (rows, count), 1)
    spread = jnp.where(row == source, 1.0, 0.0).astype(jnp.bfloat16)
    both = jnp.dot(spread, table, preferred_element_type=jnp.float32)
    slot = lax.rem(lax.broadcasted_iota(jnp.int32, (rows, lanes), 0), 8) // 4
    lane = lax.broadcasted_iota(jnp.int32, (rows, lanes), 1)
    one = jnp.where(slot == lane, both, 0.0).astype(jnp.bfloat16)
    ones = jnp.ones((lanes, lanes), jnp.bfloat16)
    return jnp.dot(one, ones, preferred_element_type=jnp.float32)


def pickers(numbers):
    rows, lanes = numbers.shape
    lane = lax.broadcasted_iota(jnp.int32, (rows, lanes), 1).astype(jnp.float32)
    quarter = lax.rem(lax.broadcasted_iota(jnp.int32, (rows, lanes), 0), 4)
    hit = jnp.where(numbers == lane, 1.0, 0.0)
    return [jnp.where(quarter == k, hit, 0.0).astype(jnp.bfloat16) for k in range(4)]


def fetch_kernel(req, table, arrived, asked, fetched, ssem, rsem):
    count = req.shape[0]
    me = lax.axis_index("dp") * 4 + lax.axis_index("rep")
    greet_all(me, count)

    def copy(src, dst, index, to):
        return pltpu.make_async_remote_copy(
            src_ref=src,
            dst_ref=dst,
            send_sem=ssem.at[index],
            recv_sem=rsem.at[index],
            device_id=to,
            device_id_type=MESH,
        )

    def ask(j, carry):
        t = lax.rem(me + j, count)
        copy(req.at[t], asked.at[me], 0, seat(t)).start()
        return carry

    lax.fori_loop(1, count, ask, 0)
    asked[pl.ds(me, 1)] = req[pl.ds(me, 1)]
    every = asked.at[pl.ds(0, count - 1)]
    copy(every, every, 0, seat(me)).wait_recv()

    group = 32

    def serve(i, carry):
        first = lax.rem(me // group + i, count // group) * group
        hits = pickers(row_numbers(asked[...], first, group))
        rows = None
        for k in range(4):
            part = jnp.dot(
                hits[k], table[:, k * BLOCK : (k + 1) * BLOCK], preferred_element_type=jnp.float32
            )
            rows = part if rows is None else rows + part
        fetched[pl.ds(first, group)] = rows.reshape(group, 8, BLOCK).astype(jnp.bfloat16)

        def hand(j, inner):
            t = first + lax.rem(me + j, group)

            @pl.when(t != me)
            def _():
                copy(fetched.at[t], arrived.at[me], 1, seat(t)).start()

            return inner

        lax.fori_loop(0, group, hand, 0)
        return carry

    lax.fori_loop(0, count // group, serve, 0)
    arrived[pl.ds(me, 1)] = fetched[pl.ds(me, 1)]
    every = req.at[pl.ds(0, count - 1)]
    copy(every, every, 0, seat(me)).wait_send()
    every = arrived.at[pl.ds(0, count - 1)]
    copy(every, every, 1, seat(me)).wait_recv()
    every = fetched.at[pl.ds(0, count - 1)]
    copy(every, every, 1, seat(me)).wait_send()


def fetch_rows(req, table):
    vmem = pl.BlockSpec(memory_space=pltpu.VMEM)
    count = req.shape[0]
    return pl.pallas_call(
        fetch_kernel,
        out_shape=(
            jax.ShapeDtypeStruct((count, 8, BLOCK), jnp.bfloat16),
            jax.ShapeDtypeStruct((count, 1, BLOCK), jnp.int32),
        ),
        in_specs=[vmem, vmem],
        out_specs=(vmem, vmem),
        scratch_shapes=[
            pltpu.VMEM((count, 8, BLOCK), jnp.bfloat16),
            pltpu.SemaphoreType.DMA((2,)),
            pltpu.SemaphoreType.DMA((2,)),
        ],
        compiler_params=pltpu.CompilerParams(collective_id=1, has_side_effects=True),
    )(req, table)


def finish_kernel(sums, returned, asked, table_out, leaf_out, in_out, out_out):
    count = asked.shape[0]
    share = 1.0 / count
    group = 64
    table_out[...] = jnp.zeros_like(table_out)

    def gather(i, carry):
        first = i * group
        hits = pickers(row_numbers(asked[...], first, group))
        rows = returned[pl.ds(first, group)].reshape(group * 8, BLOCK)
        for k in range(4):
            table_out[:, k * BLOCK : (k + 1) * BLOCK] += lax.dot_general(
                hits[k], rows, (((0,), (0,)), ((), ())), preferred_element_type=jnp.float32
            )
        return carry

    lax.fori_loop(0, count // group, gather, 0)
    width = 512

    def scale(first, dst, rows, column):
        def body(i, carry):
            at = pl.multiple_of(i * 64, 64)
            dst[pl.ds(at, 64), column : column + width] = (
                sums[pl.ds(pl.multiple_of(first + i * 64, 64), 64), :].astype(jnp.float32) * share
            )
            return carry

        lax.fori_loop(0, rows // 64, body, 0)

    for i in range(4):
        scale(i * width, in_out, width, i * width)
    scale(2048, out_out, 512, 0)
    scale(2560, leaf_out, 256, 0)


def finish(sums, returned, asked):
    vmem = pl.BlockSpec(memory_space=pltpu.VMEM)
    f32 = jnp.float32
    return pl.pallas_call(
        finish_kernel,
        out_shape=(
            jax.ShapeDtypeStruct((128, 512), f32),
            jax.ShapeDtypeStruct((256, 512), f32),
            jax.ShapeDtypeStruct((512, 2048), f32),
            jax.ShapeDtypeStruct((512, 512), f32),
        ),
        in_specs=[vmem] * 3,
        out_specs=(vmem,) * 4,
    )(sums, returned, asked)


def add_into(dst, start, sources, rows, step):
    def body(i, carry):
        total = None
        for ref, first in sources:
            part = ref[pl.ds(pl.multiple_of(first + i * step, 16), step), :].astype(jnp.float32)
            total = part if total is None else total + part
        dst[pl.ds(pl.multiple_of(start + i * step, 16), step), :] = total.astype(dst.dtype)
        return carry

    lax.fori_loop(0, rows // step, body, 0)


def sum_kernel(g, back, out, returned, w, r0, r1a, r1b, r2a, r2b, rz, ssem, rsem, bsem):
    x, y, z, c = here()
    p1 = (1 - c) * x + c * y
    p2 = c * x + (1 - c) * y

    def axis1(d):
        return device(lax.rem(x + (1 - c) * d, 4), lax.rem(y + c * d, 4), z, c)

    def axis2(d):
        return device(lax.rem(x + c * d, 4), lax.rem(y + (1 - c) * d, 4), z, c)

    def axisz(d):
        return device(x, y, lax.rem(z + d, 8), c)

    partner = device(x, y, z, 1 - c)
    count = back.shape[0]
    me = lax.axis_index("dp") * 4 + x
    greet_all(me, count)

    started = []

    def send(src, dst, index, to):
        copy = pltpu.make_async_remote_copy(
            src_ref=src,
            dst_ref=dst,
            send_sem=ssem.at[index],
            recv_sem=rsem.at[index],
            device_id=to,
            device_id_type=MESH,
        )
        copy.start()
        started.append(copy)

    def arrive(ref, index):
        pltpu.make_async_remote_copy(
            src_ref=ref,
            dst_ref=ref,
            send_sem=ssem.at[index],
            recv_sem=rsem.at[index],
            device_id=partner,
            device_id_type=MESH,
        ).wait_recv()

    base = c * HALF
    other = (1 - c) * HALF
    order = (2, 1, 3, 0)
    for k, off in enumerate(order):
        q = lax.rem(p2 + off, 4)
        send(g.at[span(other + q * R1, R1), :], r0.at[span(q * R1, R1), :], k, partner)

    def back_copy(src, dst, to):
        return pltpu.make_async_remote_copy(
            src_ref=src,
            dst_ref=dst,
            send_sem=bsem.at[0],
            recv_sem=bsem.at[1],
            device_id=to,
            device_id_type=MESH,
        )

    def give_back(j, carry):
        t = lax.rem(me + j, count)
        back_copy(back.at[t], returned.at[me], seat(t)).start()
        return carry

    lax.fori_loop(1, count, give_back, 0)
    returned[pl.ds(me, 1)] = back[pl.ds(me, 1)]

    def ring_sum(pos, first, rows, right, left, ra, rb, index, local, own):
        half = rows // 2
        q2 = lax.rem(pos + 2, 4)
        q1 = lax.rem(pos + 1, 4)
        q3 = lax.rem(pos + 3, 4)
        local(q2, 0)
        at = first + q2 * rows
        send(w.at[span(at, half), :], ra.at[0], index, right)
        send(w.at[span(at + half, half), :], ra.at[1], index + 1, left)
        local(q1, 1)
        local(q3, 2)
        arrive(ra.at[0], index)
        at = first + q1 * rows
        add_into(w, at, [(w, at), (ra.at[0], 0)], half, 48)
        send(w.at[span(at, rows), :], rb.at[0], index + 2, right)
        arrive(ra.at[1], index + 1)
        at = first + q3 * rows
        add_into(w, at + half, [(w, at + half), (ra.at[1], 0)], half, 48)
        send(w.at[span(at, rows), :], rb.at[1], index + 3, left)
        own()
        arrive(rb.at[0], index + 2)
        arrive(rb.at[1], index + 3)

    def local1(q, k):
        at = q * R1
        arrive(r0.at[span(at, R1), :], k)
        add_into(w, at, [(g, base + at), (r0, at)], R1, 48)

    w1 = p1 * R1
    ring_sum(
        p1, 0, R1, axis1(1), axis1(3), r1a, r1b, 4, local1,
        lambda: arrive(r0.at[span(w1, R1), :], 3),
    )
    add_into(w, w1, [(g, base + w1), (r0, w1), (r1b.at[0], 0), (r1b.at[1], 0)], R1, 48)
    w2 = w1 + p2 * R2
    ring_sum(
        p2, w1, R2, axis2(1), axis2(3), r2a, r2b, 8, lambda q, k: None, lambda: None
    )
    add_into(w, w2, [(w, w2), (r2b.at[0], 0), (r2b.at[1], 0)], R2, 48)

    def part(j):
        return j // 4 * RZ, lax.rem(j, 4) * 128

    for j in range(1, 8):
        row, column = part(lax.rem(z + j, 8))
        send(
            w.at[pl.ds(pl.multiple_of(w2 + row, RZ), RZ), span(column, 128)],
            rz.at[j - 1],
            11 + j,
            axisz(j),
        )
    row, column = part(z)
    total = w[pl.ds(pl.multiple_of(w2 + row, RZ), RZ), span(column, 128)].astype(jnp.float32)
    for j in range(1, 8):
        arrive(rz.at[j - 1], 11 + j)
        total = total + rz[j - 1].astype(jnp.float32)
    mine = (pl.ds(pl.multiple_of(base + w2 + row, RZ), RZ), span(column, 128))
    out[mine] = total.astype(out.dtype)
    for j in range(1, 8):
        send(out.at[mine], out.at[mine], 18 + j, axisz(j))
    for j in range(1, 8):
        row, column = part(lax.rem(z + 8 - j, 8))
        arrive(out.at[pl.ds(pl.multiple_of(base + w2 + row, RZ), RZ), span(column, 128)], 18 + j)

    def ring_share(pos, first, rows, right, left, index, ready):
        half = rows // 2
        at = first + pos * rows
        send(out.at[span(at, rows), :], out.at[span(at, rows), :], index, right)
        send(out.at[span(at, rows), :], out.at[span(at, rows), :], index + 1, left)
        ready(pos, 0)
        q = lax.rem(pos + 3, 4)
        at = first + q * rows
        arrive(out.at[span(at, rows), :], index)
        send(out.at[span(at, half), :], out.at[span(at, half), :], index + 2, right)
        ready(q, 1)
        q = lax.rem(pos + 1, 4)
        at = first + q * rows
        arrive(out.at[span(at, rows), :], index + 1)
        send(out.at[span(at + half, half), :], out.at[span(at + half, half), :], index + 3, left)
        ready(q, 2)
        q = lax.rem(pos + 2, 4)
        at = first + q * rows
        arrive(out.at[span(at, half), :], index + 2)
        arrive(out.at[span(at + half, half), :], index + 3)
        ready(q, 3)

    ring_share(p2, base + w1, R2, axis2(1), axis2(3), 26, lambda q, k: None)

    def pass_on(q, k):
        rows = out.at[span(base + q * R1, R1), :]
        send(rows, rows, 34 + k, partner)

    ring_share(p1, base, R1, axis1(1), axis1(3), 30, pass_on)
    for k, off in enumerate((0, 3, 1, 2)):
        q = lax.rem(p2 + off, 4)
        arrive(out.at[span(other + q * R1, R1), :], 34 + k)
    for copy in started:
        copy.wait_send()
    every = returned.at[pl.ds(0, count - 1)]
    back_copy(every, every, seat(me)).wait_recv()
    every = back.at[pl.ds(0, count - 1)]
    back_copy(every, every, seat(me)).wait_send()


def sum_all(g, back):
    vmem = pl.BlockSpec(memory_space=pltpu.VMEM)
    bf16 = jnp.bfloat16
    return pl.pallas_call(
        sum_kernel,
        out_shape=(
            jax.ShapeDtypeStruct((ROWS_ALL, 512), bf16),
            jax.ShapeDtypeStruct(back.shape, bf16),
        ),
        in_specs=[vmem, vmem],
        out_specs=(vmem, vmem),
        scratch_shapes=[
            pltpu.VMEM((HALF, 512), bf16),
            pltpu.VMEM((HALF, 512), bf16),
            pltpu.VMEM((2, R1 // 2, 512), bf16),
            pltpu.VMEM((2, R1, 512), bf16),
            pltpu.VMEM((2, R2 // 2, 512), bf16),
            pltpu.VMEM((2, R2, 512), bf16),
            pltpu.VMEM((7, RZ, 128), bf16),
            pltpu.SemaphoreType.DMA((38,)),
            pltpu.SemaphoreType.DMA((38,)),
            pltpu.SemaphoreType.DMA((2,)),
        ],
        compiler_params=pltpu.CompilerParams(collective_id=0, has_side_effects=True),
    )(g, back)


TILE = 128


def tn(a, b):
    return lax.dot_general(a, b, (((0,), (0,)), ((), ())), preferred_element_type=jnp.float32)


def nt(a, b):
    return lax.dot_general(a, b, (((1,), (1,)), ((), ())), preferred_element_type=jnp.float32)


def nn(a, b):
    return jnp.dot(a, b, preferred_element_type=jnp.float32)


def silu_and_slope(v):
    half = 0.5 * v
    t = jnp.tanh(half)
    up = 1.0 + t
    return half * up, 0.5 * up * (1.0 + half * (1.0 - t))


def centered(values):
    center = values - jnp.mean(values, axis=-1, keepdims=True)
    spread = jnp.mean(center * center, axis=-1, keepdims=True)
    scale = lax.rsqrt(spread + epsilon)
    return center * scale, scale


def norm_back(d, normal, scale):
    mean = jnp.mean(d, axis=-1, keepdims=True)
    along = jnp.mean(d * normal, axis=-1, keepdims=True)
    return scale * (d - mean - normal * along)


def layer_kernel(
    lengths, slots, leaves, arrived, leaf_table, w_in, w_out, cotangent,
    output, grads, back,
    pick, onehot, flat, rows, inputs, normed, scale, hidden, slope, weights, bend, mixed, gated,
    d_mixed, d_hidden, turned, d_inputs,
):
    f32, bf16 = jnp.float32, jnp.bfloat16
    count, width = output.shape
    steps = count // TILE
    head = width // HEADS

    def tile(r):
        return pl.ds(pl.multiple_of(r * TILE, TILE), TILE)

    def block(i):
        return pl.ds(pl.multiple_of(i * width, width), width)

    flat[...] = arrived[...].reshape(4 * count, 128).astype(f32)
    for k in range(4):
        rows[:, k * 128 : (k + 1) * 128] = flat[pl.ds(k, count, stride=4), :].astype(bf16)

    def build(r, carry):
        number = lax.broadcasted_iota(jnp.int32, (TILE, count), 0) + r * TILE
        pick[tile(r), :] = jnp.where(number == slots[...], 1.0, 0.0).astype(bf16)
        return carry

    lax.fori_loop(0, steps, build, 0)
    each = onehot.shape[0] // leaves.shape[0]
    for t in range(leaves.shape[0]):
        number = lax.broadcasted_iota(jnp.int32, (each, count), 0)
        hit = jnp.where(number == leaves[t : t + 1, :], 1.0, 0.0)
        onehot[t * each : (t + 1) * each, :] = hit.astype(bf16)

    def front_step(r, carry):
        at = tile(r)
        x = (tn(pick[:, at], rows[...]) + tn(onehot[:, at], leaf_table[...])).astype(bf16)
        inputs[at, :] = x
        normal, factor = centered(x.astype(f32))
        normal = normal.astype(bf16)
        normed[at, :] = normal
        scale[at, :] = factor
        for i in range(4):
            cut = slice(i * width, (i + 1) * width)
            value, bent = silu_and_slope(nn(normal, w_in[:, cut]))
            hidden[at, cut] = value.astype(bf16)
            slope[at, cut] = bent
        return carry

    lax.fori_loop(0, steps, front_step, 0)

    e1 = lengths[0, 0]
    e2 = e1 + lengths[0, 1]
    e3 = e2 + lengths[0, 2]
    spans = [(max(0, i - 2), i + 1) for i in range(steps)]
    seen = []
    for i, (low, high) in enumerate(spans):
        shape = (TILE, (high - low) * TILE)
        row = lax.broadcasted_iota(jnp.int32, shape, 0) + i * TILE
        column = lax.broadcasted_iota(jnp.int32, shape, 1) + low * TILE
        first = jnp.where(row >= e1, e1, 0)
        first = jnp.where(row >= e2, e2, first)
        first = jnp.where(row >= e3, e3, first)
        seen.append(jnp.logical_and(column >= first, column <= row))
    factor = head ** (-0.5)

    def lanes(part, h):
        return pl.ds(pl.multiple_of(part * width + h * head, head), head)

    def attend(h, carry):
        for i, (low, high) in enumerate(spans):
            at = slice(i * TILE, (i + 1) * TILE)
            keys = slice(low * TILE, high * TILE)
            wide = slice(0, (high - low) * TILE)
            scores = nt(hidden[at, lanes(2, h)], hidden[keys, lanes(3, h)]) * factor
            value, bent = silu_and_slope(scores)
            value = jnp.where(seen[i], value, 0.0).astype(bf16)
            weights[h, at, wide] = value
            bend[h, at, wide] = jnp.where(seen[i], bent * factor, 0.0)
            mixed[at, lanes(0, h)] = nn(value, hidden[keys, lanes(1, h)])
        return carry

    lax.fori_loop(0, HEADS, attend, 0)

    def middle(r, carry):
        at = tile(r)
        normal, factor = centered(mixed[at, :])
        gates = hidden[at, 0:width].astype(f32)
        gate = (normal * gates).astype(bf16)
        gated[at, :] = gate
        output[at, :] = (nn(gate, w_out[...]) + inputs[at, :].astype(f32)).astype(bf16)
        d_gated = nt(cotangent[at, :], w_out[...]).astype(bf16).astype(f32)
        d_gates = (d_gated * normal).astype(bf16).astype(f32)
        d_hidden[at, 0:width] = (d_gates * slope[at, 0:width]).astype(bf16)
        d_mixed[at, :] = norm_back(d_gated * gates, normal, factor).astype(bf16)
        return carry

    lax.fori_loop(0, steps, middle, 0)

    def attend_back(h, carry):
        d_keys = [None] * steps
        d_values = [None] * steps
        for i, (low, high) in enumerate(spans):
            at = slice(i * TILE, (i + 1) * TILE)
            keys = slice(low * TILE, high * TILE)
            wide = slice(0, (high - low) * TILE)
            d_mix = d_mixed[at, lanes(0, h)]
            d_weights = nt(d_mix, hidden[keys, lanes(1, h)]).astype(bf16).astype(f32)
            d_scores = (d_weights * bend[h, at, wide]).astype(bf16)
            d_queries = nn(d_scores, hidden[keys, lanes(3, h)]).astype(bf16).astype(f32)
            d_hidden[at, lanes(2, h)] = (d_queries * slope[at, lanes(2, h)]).astype(bf16)
            dk = tn(d_scores, hidden[at, lanes(2, h)])
            dv = tn(weights[h, at, wide], d_mix)
            for j in range(low, high):
                cut = slice((j - low) * TILE, (j - low + 1) * TILE)
                d_keys[j] = dk[cut] if d_keys[j] is None else d_keys[j] + dk[cut]
                d_values[j] = dv[cut] if d_values[j] is None else d_values[j] + dv[cut]
        for j in range(steps):
            at = slice(j * TILE, (j + 1) * TILE)
            for part, total in ((3, d_keys[j]), (1, d_values[j])):
                total = total.astype(bf16).astype(f32)
                d_hidden[at, lanes(part, h)] = (total * slope[at, lanes(part, h)]).astype(bf16)
        return carry

    lax.fori_loop(0, HEADS, attend_back, 0)

    turned[...] = normed[...].T

    def weight_step(r, carry):
        at = tile(r)
        for i in range(4):
            cut = slice(i * width, (i + 1) * width)
            grads[pl.ds(pl.multiple_of(i * width + r * TILE, TILE), TILE), :] = nn(
                turned[at, :], d_hidden[:, cut]
            ).astype(bf16)
        d_normed = nt(d_hidden[at, :], w_in[...]).astype(bf16).astype(f32)
        x = inputs[at, :].astype(f32)
        normal = (x - jnp.mean(x, axis=-1, keepdims=True)) * scale[at, :]
        d = norm_back(d_normed, normal, scale[at, :])
        d_inputs[at, :] = (d + cotangent[at, :].astype(f32)).astype(bf16)
        return carry

    lax.fori_loop(0, steps, weight_step, 0)
    turned[...] = gated[...].T

    def last_step(r, carry):
        at = tile(r)
        grads[pl.ds(pl.multiple_of(4 * width + r * TILE, TILE), TILE), :] = nn(
            turned[at, :], cotangent[...]
        ).astype(bf16)
        d_rows = nn(pick[at, :], d_inputs[...])
        for k in range(4):
            flat[pl.ds(r * 4 * TILE + k, TILE, stride=4), :] = d_rows[:, k * 128 : (k + 1) * 128]
        return carry

    lax.fori_loop(0, steps, last_step, 0)
    grads[5 * width : 5 * width + onehot.shape[0], :] = nn(onehot[...], d_inputs[...]).astype(bf16)
    grads[5 * width + onehot.shape[0] :, :] = jnp.zeros(
        (grads.shape[0] - 5 * width - onehot.shape[0], width), bf16
    )
    back[...] = flat[...].astype(bf16).reshape(back.shape)


def layer(lengths, slots, leaves, arrived, leaf_table, w_in, w_out, cotangent):
    f32, bf16 = jnp.float32, jnp.bfloat16
    count, width = cotangent.shape
    vmem = pl.BlockSpec(memory_space=pltpu.VMEM)
    smem = pl.BlockSpec(memory_space=pltpu.SMEM)
    return pl.pallas_call(
        layer_kernel,
        out_shape=(
            jax.ShapeDtypeStruct((count, width), bf16),
            jax.ShapeDtypeStruct((ROWS_ALL, width), bf16),
            jax.ShapeDtypeStruct(arrived.shape, bf16),
        ),
        in_specs=[smem] + [vmem] * 7,
        out_specs=(vmem,) * 3,
        scratch_shapes=[
            pltpu.VMEM((count, count), bf16),
            pltpu.VMEM((leaf_table.shape[0], count), bf16),
            pltpu.VMEM((4 * count, 128), f32),
            pltpu.VMEM((count, width), bf16),
            pltpu.VMEM((count, width), bf16),
            pltpu.VMEM((count, width), bf16),
            pltpu.VMEM((count, 1), f32),
            pltpu.VMEM((count, 4 * width), bf16),
            pltpu.VMEM((count, 4 * width), f32),
            pltpu.VMEM((HEADS, count, 3 * TILE), bf16),
            pltpu.VMEM((HEADS, count, 3 * TILE), f32),
            pltpu.VMEM((count, width), f32),
            pltpu.VMEM((count, width), bf16),
            pltpu.VMEM((count, width), bf16),
            pltpu.VMEM((count, 4 * width), bf16),
            pltpu.VMEM((width, count), bf16),
            pltpu.VMEM((count, width), bf16),
        ],
    )(lengths, slots, leaves, arrived, leaf_table, w_in, w_out, cotangent)


def on_device(
    item_table, requests, event_slot, lengths, leaf_ids, leaf_table, w_in, w_out, cotangent
):
    count = requests.shape[1]
    asks = jnp.pad(requests.reshape(count, 1, 2), ((0, 0), (0, 0), (0, BLOCK - 2)))
    blocks, asked = fetch_rows(asks, item_table)
    output, grads, d_blocks = layer(
        lengths,
        event_slot.reshape(1, -1),
        leaf_ids.T,
        blocks,
        leaf_table,
        w_in,
        w_out,
        cotangent,
    )
    sums, returned = sum_all(grads, d_blocks)
    return (output, *finish(sums, returned, asked))


def solution(mesh):
    return jax.shard_map(
        on_device,
        mesh=mesh,
        in_specs=(
            P(("dp", "rep"), None),
            P(("dp", "rep"), None, None),
            P(("dp", "rep")),
            P(("dp", "rep"), None),
            P(("dp", "rep"), None),
            P(),
            P(),
            P(),
            P(("dp", "rep"), None),
        ),
        out_specs=(P(("dp", "rep"), None), P(("dp", "rep"), None), P(), P(), P()),
        check_vma=False,
    )
```
